512 devices in a mesh: section: 4 (over x), expert: 64 (over z, y), pair: 2 (over core).
Axes of the slice: x: 4, y: 8, z: 8, core: 2. Of those that a mesh axis runs over, the one named last changes fastest.
Arguments:
- initial_state: bfloat16 [32768, 2048], P(('section', 'expert')), may hold values from -6 to 6
- prelude: bfloat16 [32768, 2048], P(('section', 'expert')), may hold values from -6 to 6
- inject_gain: float32 [2048], replicated, may hold values from 0.1 to 1.9
- norm_gain: float32 [2048], replicated, may hold values from 0.1 to 1.9
- router: bfloat16 [2048, 64], replicated, may hold values from -0.125 to 0.125
- gate_w: bfloat16 [64, 2048, 1024], P('expert', 'section', 'pair'), may hold values from -0.125 to 0.125
- up_w: bfloat16 [64, 2048, 1024], P('expert', 'section', 'pair'), may hold values from -0.125 to 0.125
- down_w: bfloat16 [64, 1024, 2048], P('expert', 'pair', 'section'), may hold values from -0.1875 to 0.1875
- routes: int32 [1, 32768, 8], P(None, ('section', 'expert')), may hold values from 0 to 63, all different within a row; in each aligned block of 128 rows (0 to 127, 128 to 255, ..., all dimensions but the last counted through in order) at most 18 rows name the same one
Outputs:
- final_state: bfloat16 [32768, 2048], P(('section', 'expert'), 'pair')
The draws below stay inside these ranges and needn't reach their ends.
Inputs may be any that keep to these rules, and one draw needn't show every extreme that they name: `routes`: each row names 8 different experts. Within the 128 rows of one device in one pass (aligned blocks of the token dimension), no expert is named more than 18 times, a bound that some block reaches.
All inputs are finite; a program needn't handle non-finite values.
Results may differ from the reference program's by a relative error of at most 0.0029.
Values may be sent and summed in bfloat16 or wider, within the bound.
No kernel may reach another device: no remote copies, remote signals or barrier semaphores. Data moves between devices by JAX's collectives and lax.ppermute only.
A program may use at most 64 MiB of HBM per device.

```python
import math
import jax
import jax.numpy as jnp
import numpy as np
from jax import lax

D = 2048
HID = 1024
EXPERTS = 64
TOPK = 8
TOK_DEV = 128
LOOPS = 1
CAP = 18
TOKENS = 32768
N_PAIR = 2


def level_of(key, shape, cuts, low, high):
    def one(position, shards_of):
        heights = jax.random.uniform(jax.random.fold_in(jax.random.fold_in(key, 6), position), (shards_of,), jnp.float32, low / len(cuts), high / len(cuts))
        return jnp.repeat(jnp.exp(heights), shape[position] // shards_of).reshape((-1,) + (1,) * (len(shape) - position - 1))

    loudness = one(*cuts[0])
    for cut in cuts[1:]:
        loudness = loudness * one(*cut)
    return loudness


def assign_block(rng, own, number, rows, count, top, reach, skew):
    order = jax.random.permutation(rng, count)
    heavy_load, usual = load_shares(count, rows * top, reach, skew, True), load_shares(count, rows * top, reach, skew, False)
    places = jnp.arange(count)

    def named(sizes, turn):
        used = int((sizes > 0).sum())
        fixed = max(1, used // 4)
        moved = fixed + (places - fixed + turn * (used - fixed)) % max(1, count - fixed)
        return jnp.zeros((count,), jnp.int32).at[order[jnp.where(places < fixed, places, moved)]].set(jnp.asarray(sizes, jnp.int32))

    sizes = jnp.where(number % 4 == 0, named(heavy_load, number // 4), named(usual, number - number // 4 - 1))
    mixed = jax.random.permutation(jax.random.fold_in(own, 3), count)
    source_of, sink = mixed[0:count // 2 * 2:2], mixed[1:count // 2 * 2:2]
    margin = jnp.minimum(sizes[source_of] - 1, reach - sizes[sink]) // 2
    margin = jnp.where((source_of == order[0]) | (sink == order[0]) | (sizes[sink] == 0), 0, jnp.maximum(margin, 0))
    moved = jax.random.randint(jax.random.fold_in(own, 4), (count // 2,), 0, 1 << 20) % (margin + 1)
    sizes = sizes.at[source_of].add(-moved).at[sink].add(moved)
    members = jnp.searchsorted(jnp.cumsum(sizes), jnp.arange(rows * top), side="right").astype(jnp.int32)
    listing = members.reshape(top, rows).T
    listing = listing[jax.random.permutation(jax.random.fold_in(own, 1), rows)]
    turn = jax.random.randint(jax.random.fold_in(own, 2), (rows, 1), 0, top)
    return jnp.take_along_axis(listing, (jnp.arange(top)[None, :] + turn) % top, axis=1)


def load_shares(count, total, bound, lean, full):
    portions = [(1 << 20) // math.isqrt(standing ** lean) + 1 for standing in range(1, count + 1)]
    largest = bound if full else min(bound, max(-(-total // count), total * portions[0] // sum(portions)))
    least = 1 if total - largest >= count - 1 else 0
    counts, spare = [largest] + [least] * (count - 1), total - largest - least * (count - 1)
    while spare > 0:
        movable = [i for i in range(1, count) if counts[i] < largest] or [i for i in range(1, count) if counts[i] < bound]
        pool, budget = sum([portions[i] for i in movable]), spare
        for i in movable:
            extra = min(bound - counts[i], max(1, budget * portions[i] // pool), spare)
            counts[i] = counts[i] + extra
            spare = spare - extra
    return np.array(counts)


def bell_draw(stream_key, shape, width, most, split=(), held_as=jnp.bfloat16):
    array = width * jax.random.normal(stream_key, shape, jnp.float32)
    if split:
        array = array * level_of(stream_key, shape, split, -0.22, 0.18)
    return jnp.clip(array, -most, most).astype(held_as)


def setup_inputs(seed: int = 0) -> dict:
    keys = jax.random.split(jax.random.key(seed), 10)
    initial_state = bell_draw(keys[0], (TOKENS, D), 1.0, 6.0, ((0, 256),))
    prelude = bell_draw(keys[1], (TOKENS, D), 1.0, 6.0, ((0, 256),))
    inject_gain = jnp.clip(1.0 + 0.18 * jax.random.normal(keys[2], (D,), jnp.float32), 0.1, 1.9)
    norm_gain = jnp.clip(1.0 + 0.18 * jax.random.normal(keys[3], (D,), jnp.float32), 0.1, 1.9)
    router = bell_draw(keys[4], (D, EXPERTS), D ** -0.5, 0.125)
    gate_w = bell_draw(keys[5], (EXPERTS, D, HID), D ** -0.5, 0.125, ((0, 64), (1, 4), (2, 2)))
    up_w = bell_draw(keys[6], (EXPERTS, D, HID), D ** -0.5, 0.125, ((0, 64), (1, 4), (2, 2)))
    down_w = bell_draw(keys[7], (EXPERTS, HID, D), HID ** -0.5, 0.1875, ((0, 64), (1, 2), (2, 4)))
    routes_keys = jax.random.split(jax.random.fold_in(keys[8], 1), LOOPS * TOKENS // TOK_DEV)
    routes_turns = jax.random.permutation(jax.random.fold_in(keys[8], 3), LOOPS * TOKENS // TOK_DEV)
    routes = jax.vmap(lambda own, number: assign_block(jax.random.fold_in(keys[8], 2), own, number, TOK_DEV, EXPERTS, TOPK, CAP, 2))(routes_keys, routes_turns).reshape((LOOPS, TOKENS, TOPK))
    return {"initial_state": initial_state, "prelude": prelude, "inject_gain": inject_gain, "norm_gain": norm_gain, "router": router, "gate_w": gate_w, "up_w": up_w, "down_w": down_w, "routes": routes}


def reference(initial_state, prelude, inject_gain, norm_gain, router, gate_w, up_w, down_w, routes):
    hidden_state = initial_state.astype(jnp.float32)
    prelude_f = prelude.astype(jnp.float32)
    block_count = TOKENS // TOK_DEV
    half_width = HID // N_PAIR
    token_ids = jnp.broadcast_to(jnp.arange(TOKENS, dtype=jnp.int32).reshape(block_count, TOK_DEV, 1), (block_count, TOK_DEV, TOPK)).reshape(-1)
    block_ids = jnp.broadcast_to(jnp.arange(block_count, dtype=jnp.int32)[:, None], (block_count, TOK_DEV * TOPK))
    for pass_index in range(LOOPS):
        mixed_state = hidden_state + prelude_f * inject_gain
        inv_rms = lax.rsqrt(lax.optimization_barrier(jnp.mean(mixed_state * mixed_state, axis=-1, keepdims=True)) + 1e-06)
        normed = (mixed_state * inv_rms * norm_gain).astype(jnp.bfloat16)
        logits = jnp.dot(normed, router, preferred_element_type=jnp.float32)
        router_prob = jax.nn.sigmoid(logits)
        chosen = routes[pass_index]
        picked = jnp.take_along_axis(router_prob, chosen, axis=1)
        gate_vals = picked / lax.optimization_barrier(jnp.sum(picked, axis=1, keepdims=True))
        flat_ids = chosen.reshape(block_count, TOK_DEV * TOPK)
        onehot = (flat_ids[:, :, None] == jnp.arange(EXPERTS, dtype=jnp.int32)).astype(jnp.int32)
        before = jnp.cumsum(onehot, axis=1) - onehot
        slot_rank = lax.optimization_barrier(jnp.sum(before * onehot, axis=-1))
        column = (block_ids * CAP + slot_rank).reshape(-1).astype(jnp.int32)
        expert_ids = flat_ids.reshape(-1).astype(jnp.int32)
        slot_table = jnp.full((EXPERTS, block_count * CAP), TOKENS, jnp.int32).at[expert_ids, column].set(token_ids)
        weight_table = jnp.zeros((EXPERTS, block_count * CAP), jnp.float32).at[expert_ids, column].set(gate_vals.reshape(-1))
        padded_rows = jnp.concatenate([normed, jnp.zeros((1, D), jnp.bfloat16)], axis=0)

        def one_expert(moe_total, expert_items):
            slot_row, weight_row, gate_one, up_one, down_one = expert_items
            row_block = padded_rows[slot_row]
            gate_act = jnp.dot(row_block, gate_one, preferred_element_type=jnp.float32)
            up_act = jnp.dot(row_block, up_one, preferred_element_type=jnp.float32)
            inner_act = (jax.nn.silu(gate_act) * up_act).astype(jnp.bfloat16)
            result = jnp.zeros((row_block.shape[0], D), jnp.float32)
            for half_index in range(N_PAIR):
                half_part = jnp.dot(inner_act[:, half_index * half_width:(half_index + 1) * half_width], down_one[half_index * half_width:(half_index + 1) * half_width], preferred_element_type=jnp.float32).astype(jnp.bfloat16)
                result = result + half_part.astype(jnp.float32)
            result = result.astype(jnp.bfloat16).astype(jnp.float32)
            moe_total = moe_total.at[slot_row].add(weight_row[:, None] * result, mode='drop')
            return (moe_total, None)
        moe_out = lax.scan(one_expert, jnp.zeros((TOKENS, D), jnp.float32), (slot_table, weight_table, gate_w, up_w, down_w))[0]
        hidden_state = mixed_state + moe_out
    return hidden_state.astype(jnp.bfloat16)
```

```python
import jax
import jax.numpy as jnp
from jax import lax
from jax.experimental import pallas as pl
from jax.experimental.pallas import tpu as pltpu
from jax.sharding import PartitionSpec as P


TOPK = 8
CAP = 18
MAIN = 8
HALF_CAP = CAP // 2
LANES = 128
F32 = jnp.float32
BF16 = jnp.bfloat16
VMEM = pl.BlockSpec(memory_space=pltpu.VMEM)
SMEM = pl.BlockSpec(memory_space=pltpu.SMEM)
FAR = pl.BlockSpec(memory_space=pltpu.HBM)


def dot(a, b):
    return jnp.dot(a, b, preferred_element_type=F32)


def dot_t(a, b):
    return lax.dot_general(a, b, (((0,), (0,)), ((), ())), preferred_element_type=F32)


def route_kernel(where_ref, *refs):
    stored, refs = refs[:6], refs[6:]
    send_ref, main_hi_ref, main_lo_ref, last_hi_ref, last_lo_ref = refs[:5]
    held, sems = refs[5:11], refs[11]
    copies = [pltpu.make_async_copy(stored[i], held[i], sems.at[i]) for i in range(6)]
    for copy in copies:
        copy.start()
    for copy in copies:
        copy.wait()
    state_ref, prelude_ref, inject_ref, gain_ref, router_ref, routes_ref = held
    tokens, width = state_ref.shape
    experts = router_ref.shape[0]
    blocks = width // LANES
    low = where_ref[0] * HALF_CAP
    mixed = state_ref[...].astype(F32) + prelude_ref[...].astype(F32) * inject_ref[...]
    inv_rms = lax.rsqrt(jnp.mean(mixed * mixed, axis=-1, keepdims=True) + 1e-06)
    normed = (mixed * inv_rms * gain_ref[...]).astype(BF16)
    logits = lax.dot_general(
        normed, router_ref[...], (((1,), (1,)), ((), ())), preferred_element_type=F32
    )
    prob = jax.nn.sigmoid(logits)
    routes = routes_ref[...].astype(F32).T.astype(jnp.int32)
    expert = lax.broadcasted_iota(jnp.int32, (tokens, experts), 1)
    chosen = routes[:, 0:1] == expert
    for k in range(1, TOPK):
        chosen = jnp.logical_or(chosen, routes[:, k : k + 1] == expert)
    chosen_f = chosen.astype(F32)
    earlier = lax.broadcasted_iota(jnp.int32, (tokens, tokens), 1) < lax.broadcasted_iota(
        jnp.int32, (tokens, tokens), 0
    )
    rank = dot(earlier.astype(F32).astype(BF16), chosen_f.astype(BF16))
    place = jnp.where(chosen, rank + 1.0, 0.0)
    picked = chosen_f * prob
    gate = picked / jnp.sum(picked, axis=1, keepdims=True)
    gate_hi = gate.astype(BF16)
    gate_lo = (gate - gate_hi.astype(F32)).astype(BF16)
    lane = lax.broadcasted_iota(jnp.int32, (experts, experts * MAIN), 1)
    row = lax.broadcasted_iota(jnp.int32, (experts, experts * MAIN), 0)
    spread = (lane // MAIN == row).astype(F32).astype(BF16)
    slot = lax.broadcasted_iota(jnp.int32, (tokens, experts * MAIN), 1) % MAIN + (1 + low)
    at_main = dot(place.astype(BF16), spread) == slot.astype(F32)
    at_last = place == (low + HALF_CAP).astype(F32)
    main_hi_ref[...] = jnp.where(at_main, dot(gate_hi, spread), 0.0).astype(BF16)
    main_lo_ref[...] = jnp.where(at_main, dot(gate_lo, spread), 0.0).astype(BF16)
    last_hi_ref[...] = jnp.where(at_last, gate_hi.astype(F32), 0.0).astype(BF16)
    last_lo_ref[...] = jnp.where(at_last, gate_lo.astype(F32), 0.0).astype(BF16)
    pick_main = at_main.astype(F32).astype(BF16)
    pick_last = at_last.astype(F32).astype(BF16)
    for pair in range(blocks // 2):
        cols = normed[:, pair * 2 * LANES : (pair + 1) * 2 * LANES]
        rows = dot_t(pick_main, cols)
        for j in range(2):
            c = 2 * pair + j
            send_ref[:, c * MAIN : (c + 1) * MAIN, :] = (
                rows[:, j * LANES : (j + 1) * LANES].reshape(experts, MAIN, LANES).astype(BF16)
            )
    last = dot_t(pick_last, normed)
    send_ref[:, blocks * MAIN :, :] = last.reshape(experts, blocks, LANES).astype(BF16)


def ffn_kernel(where_ref, rows_ref, *refs):
    stored, back_ref, x_ref, act_ref = refs[:10], refs[10], refs[11], refs[12]
    weights, sems = refs[13:23], refs[23]
    sections, _, part = x_ref.shape
    experts = rows_ref.shape[0]
    blocks = sections * part // LANES
    per = part // LANES
    main = experts * MAIN
    here = where_ref[1]
    step = 256
    copies = [
        pltpu.make_async_copy(stored[i], weights[i], sems.at[i]) for i in range(len(stored))
    ]
    for copy in copies:
        copy.start()
    last = rows_ref[:, blocks * MAIN :, :].astype(F32).reshape(experts, blocks * LANES)
    for s in range(sections):
        for c in range(per):
            b = s * per + c
            x_ref[s, :main, c * LANES : (c + 1) * LANES] = (
                rows_ref[:, b * MAIN : (b + 1) * MAIN, :].reshape(main, LANES)
            )
        x_ref[s, main:, :] = last[:, s * part : (s + 1) * part].astype(BF16)
    offsets = (0, 1, 3, 2)
    at = [lax.rem(here + d, sections) for d in offsets]

    def piece(q, d, first, size, cols):
        own = weights[q * 5 : q * 5 + 5]
        if offsets[d] != 2:
            return own[d][first : first + size, cols]
        edge = own[3].shape[0]
        if first + size <= edge:
            return own[3][first : first + size, cols]
        return own[4][first - edge : first - edge + size, cols]

    for q in range(2):
        for copy in copies[q * 5 : q * 5 + 5]:
            copy.wait()
        for n in range(part // step):
            cols = slice(n * step, (n + 1) * step)
            total = [None, None]
            for which in range(2):
                for d in range(sections):
                    for k in range(part // step):
                        term = dot(
                            x_ref[at[d], :, k * step : (k + 1) * step],
                            piece(q, d, which * part + k * step, step, cols),
                        )
                        total[which] = term if total[which] is None else total[which] + term
            act = jax.nn.silu(total[0]) * total[1]
            act_ref[:, q * part + n * step : q * part + (n + 1) * step] = act.astype(BF16)
    for d in range(sections):
        wide = []
        for n in range(part // step):
            cols = slice(n * step, (n + 1) * step)
            total = None
            for q in range(2):
                partial = None
                for k in range(part // step):
                    term = dot(
                        act_ref[:, q * part + k * step : q * part + (k + 1) * step],
                        piece(q, d, 2 * part + k * step, step, cols),
                    )
                    partial = term if partial is None else partial + term
                partial = partial.astype(BF16).astype(F32)
                total = partial if total is None else total + partial
            for j in range(step // LANES):
                b = at[d] * per + n * (step // LANES) + j
                back_ref[:, pl.ds(pl.multiple_of(b * MAIN, MAIN), MAIN), :] = (
                    total[:main, j * LANES : (j + 1) * LANES]
                    .reshape(experts, MAIN, LANES)
                    .astype(BF16)
                )
            wide.append(total[main:])
        x_ref[at[d], main:, :] = jnp.concatenate(wide, axis=1).astype(BF16)
    whole = jnp.concatenate([x_ref[s, main:, :] for s in range(sections)], axis=1)
    back_ref[:, blocks * MAIN :, :] = (
        whole.astype(F32).reshape(experts, blocks, LANES).astype(BF16)
    )


def combine_half(half, rows_ref, main_hi, main_lo, last_hi, last_lo):
    experts = rows_ref.shape[0]
    blocks = rows_ref.shape[1] // HALF_CAP
    mine = blocks // 2
    main = experts * MAIN
    outs = []
    for pair in range(mine // 2):
        cols = []
        for j in range(2):
            b = half * mine + pair * 2 + j
            cols.append(
                rows_ref[:, pl.ds(pl.multiple_of(b * MAIN, MAIN), MAIN), :].reshape(main, LANES)
            )
        rows = jnp.concatenate(cols, axis=1)
        outs.append(dot(main_hi, rows) + dot(main_lo, rows))
    total = jnp.concatenate(outs, axis=1)
    first = pl.multiple_of(blocks * MAIN + half * mine, MAIN)
    last = rows_ref[:, pl.ds(first, mine), :].astype(F32)
    last = last.reshape(experts, mine * LANES).astype(BF16)
    return total + dot(last_hi, last) + dot(last_lo, last)


def send_half_kernel(where_ref, rows_ref, mh_ref, ml_ref, lh_ref, ll_ref, out_ref):
    out_ref[...] = combine_half(
        1 - where_ref[0], rows_ref, mh_ref[...], ml_ref[...], lh_ref[...], ll_ref[...]
    ).astype(BF16)


def keep_half_kernel(
    where_ref, rows_ref, mh_ref, ml_ref, lh_ref, ll_ref, state_ref, prelude_ref, inject_ref, out_ref
):
    width = out_ref.shape[1]
    half = where_ref[0]
    moe = combine_half(half, rows_ref, mh_ref[...], ml_ref[...], lh_ref[...], ll_ref[...])
    cols = pl.ds(pl.multiple_of(half * width, width), width)
    mixed = state_ref[:, cols].astype(F32) + prelude_ref[:, cols].astype(F32) * inject_ref[:, cols]
    out_ref[...] = mixed + moe


def call(kernel, outs, n_in, scratch=(), limit=10, cost=None, far=0):
    return pl.pallas_call(
        kernel,
        out_shape=outs,
        in_specs=[SMEM] + [VMEM] * (n_in - 1 - far) + [FAR] * far,
        out_specs=jax.tree.map(lambda _: VMEM, outs),
        scratch_shapes=list(scratch),
        cost_estimate=cost,
        compiler_params=pltpu.CompilerParams(vmem_limit_bytes=limit << 20),
    )


def one_pass(initial_state, prelude, inject_gain, norm_gain, router, gate_w, up_w, down_w, routes):
    tokens, width = initial_state.shape
    experts = router.shape[1]
    blocks = width // LANES
    sections = lax.axis_size("section")
    part = gate_w.shape[1]
    where = jnp.stack([lax.axis_index("pair"), lax.axis_index("section")]).astype(jnp.int32)
    inject = inject_gain[None, :]
    shape = jax.ShapeDtypeStruct

    up_ring = [(i, (i + 1) % sections) for i in range(sections)]
    down_ring = [(i, (i - 1) % sections) for i in range(sections)]
    swap = [(0, 1), (1, 0)]
    own = jnp.concatenate([gate_w[0], up_w[0], down_w[0]], axis=0)
    before = lax.ppermute(own, "section", up_ring)
    after = lax.ppermute(own, "section", down_ring)
    cut = own.shape[0] // 2
    far_a = lax.ppermute(before[:cut], "section", up_ring)
    far_b = lax.ppermute(after[cut:], "section", down_ring)
    mine = [own, after, before, far_a, far_b]
    other = [lax.ppermute(w, "pair", swap) for w in mine]

    message = shape((experts, blocks * HALF_CAP, LANES), BF16)
    send, main_hi, main_lo, last_hi, last_lo = call(
        route_kernel,
        (message,) + (shape((tokens, experts * MAIN), BF16),) * 2 + (shape((tokens, experts), BF16),) * 2,
        7,
        scratch=[
            pltpu.VMEM((tokens, width), BF16),
            pltpu.VMEM((tokens, width), BF16),
            pltpu.VMEM((1, width), F32),
            pltpu.VMEM((1, width), F32),
            pltpu.VMEM((experts, width), BF16),
            pltpu.VMEM((TOPK, tokens), jnp.int32),
            pltpu.SemaphoreType.DMA((6,)),
        ],
        limit=60,
        far=6,
    )(where, initial_state, prelude, inject, norm_gain[None, :], router.T, routes[0].T)
    received = lax.all_to_all(send, "expert", split_axis=0, concat_axis=0, tiled=True)
    back = call(
        ffn_kernel,
        message,
        12,
        scratch=[
            pltpu.VMEM((sections, experts * HALF_CAP, part), BF16),
            pltpu.VMEM((experts * HALF_CAP, 2 * part), BF16),
            *[pltpu.VMEM(w.shape, BF16) for w in mine + other],
            pltpu.SemaphoreType.DMA((len(mine + other),)),
        ],
        limit=60,
        far=len(mine + other),
    )(where, received, *mine, *other)
    returned = lax.all_to_all(back, "expert", split_axis=0, concat_axis=0, tiled=True)
    weights = (main_hi, main_lo, last_hi, last_lo)
    half = width // 2
    given = call(send_half_kernel, shape((tokens, half), BF16), 6)(where, returned, *weights)
    got = lax.ppermute(given, "pair", swap)
    kept = call(keep_half_kernel, shape((tokens, half), F32), 9)(
        where, returned, *weights, initial_state, prelude, inject
    )
    return (kept + got.astype(F32)).astype(BF16)


def solution(mesh):
    placed = (
        P(("section", "expert"), None),
        P(("section", "expert"), None),
        P(),
        P(),
        P(),
        P("expert", "section", "pair"),
        P("expert", "section", "pair"),
        P("expert", "pair", "section"),
        P(None, ("section", "expert"), None),
    )
    return jax.shard_map(
        one_pass,
        mesh=mesh,
        in_specs=placed,
        out_specs=P(("section", "expert"), "pair"),
        check_vma=False,
    )
```

```python
import jax
import jax.numpy as jnp
from jax import lax
from jax.experimental import pallas as pl
from jax.experimental.pallas import tpu as pltpu
from jax.sharding import PartitionSpec as P


TOPK = 8
CAP = 18
MAIN = 8
HALF_CAP = CAP // 2
LANES = 128
AHEAD = 4
WHOLE = 67_000_000
F32 = jnp.float32
BF16 = jnp.bfloat16
VMEM = pl.BlockSpec(memory_space=pltpu.VMEM)
FAR = pl.BlockSpec(memory_space=pltpu.HBM)


def dot(a, b):
    return jnp.dot(a, b, preferred_element_type=F32)


def dot_t(a, b):
    return lax.dot_general(a, b, (((0,), (0,)), ((), ())), preferred_element_type=F32)


def normalize(state, prelude, inject, gain):
    mixed = state.astype(F32) + prelude.astype(F32) * inject
    inv_rms = lax.rsqrt(jnp.mean(mixed * mixed, axis=-1, keepdims=True) + 1e-06)
    return (mixed * inv_rms * gain).astype(BF16)


def places(routes, experts):
    routes = routes.astype(F32).T.astype(jnp.int32)
    tokens = routes.shape[0]
    expert = lax.broadcasted_iota(jnp.int32, (tokens, experts), 1)
    chosen = routes[:, 0:1] == expert
    for k in range(1, TOPK):
        chosen = jnp.logical_or(chosen, routes[:, k : k + 1] == expert)
    earlier = lax.broadcasted_iota(jnp.int32, (tokens, tokens), 1) < lax.broadcasted_iota(
        jnp.int32, (tokens, tokens), 0
    )
    rank = dot(earlier.astype(F32).astype(BF16), chosen.astype(F32).astype(BF16))
    return jnp.where(chosen, rank + 1.0, 0.0)


def widen(rows, times):
    lane = lax.broadcasted_iota(jnp.int32, (rows, rows * times), 1)
    row = lax.broadcasted_iota(jnp.int32, (rows, rows * times), 0)
    return (lane // times == row).astype(F32).astype(BF16)


def route_kernel(*refs):
    stored, parts, out_ref, own_refs = refs[:5], refs[5:8], refs[8], refs[9:11]
    held, send_ref, pack_ref, sems, pack_sems, out_sems, own_sems = (
        refs[11:16], refs[16], refs[17], refs[18], refs[19], refs[20], refs[21],
    )
    copies = [pltpu.make_async_copy(stored[i], held[i], sems.at[i]) for i in range(5)]
    for copy in copies:
        copy.start()
    size = parts[0].shape[0]
    packs = [
        pltpu.make_async_copy(parts[i], pack_ref.at[i * size : (i + 1) * size], pack_sems.at[i])
        for i in range(3)
    ]
    for copy in packs:
        copy.start()
    routes_ref, state_ref, prelude_ref, inject_ref, gain_ref = held
    width = state_ref.shape[1]
    experts = send_ref.shape[0]
    blocks = width // LANES
    low = lax.axis_index("pair").astype(jnp.int32) * HALF_CAP
    copies[0].wait()
    place = places(routes_ref[...], experts)
    slot = lax.broadcasted_iota(jnp.int32, (place.shape[0], experts * MAIN), 1) % MAIN + (1 + low)
    at_main = dot(place.astype(BF16), widen(experts, MAIN)) == slot.astype(F32)
    at_last = place == (low + HALF_CAP).astype(F32)
    pick_main = at_main.astype(F32).astype(BF16)
    pick_last = at_last.astype(F32).astype(BF16)
    for copy in copies[1:]:
        copy.wait()
    normed = normalize(state_ref[...], prelude_ref[...], inject_ref[...], gain_ref[...])
    outs = []

    def give(first, size):
        copy = pltpu.make_async_copy(
            send_ref.at[:, first : first + size, :],
            out_ref.at[:, first : first + size, :],
            out_sems.at[len(outs)],
        )
        copy.start()
        outs.append(copy)

    last = dot_t(pick_last, normed)
    send_ref[:, blocks * MAIN :, :] = last.reshape(experts, blocks, LANES).astype(BF16)
    give(blocks * MAIN, blocks)
    for pair in range(blocks // 2):
        cols = normed[:, pair * 2 * LANES : (pair + 1) * 2 * LANES]
        rows = dot_t(pick_main, cols)
        for j in range(2):
            c = 2 * pair + j
            send_ref[:, c * MAIN : (c + 1) * MAIN, :] = (
                rows[:, j * LANES : (j + 1) * LANES].reshape(experts, MAIN, LANES).astype(BF16)
            )
        give(pair * 2 * MAIN, 2 * MAIN)
        if pair == 0:
            for copy in packs:
                copy.wait()
            cut = own_refs[0].shape[0]
            owns = [
                pltpu.make_async_copy(
                    pack_ref.at[i * cut : (i + 1) * cut], own_refs[i], own_sems.at[i]
                )
                for i in range(2)
            ]
            for copy in owns:
                copy.start()
    for copy in owns:
        copy.wait()
    for copy in outs:
        copy.wait()


def gate_kernel(
    routes_ref, state_ref, prelude_ref, inject_ref, gain_ref, router_ref,
    main_hi_ref, main_lo_ref, last_hi_ref, last_lo_ref,
):
    experts = router_ref.shape[0]
    place = places(routes_ref[...], experts)
    normed = normalize(state_ref[...], prelude_ref[...], inject_ref[...], gain_ref[...])
    logits = lax.dot_general(
        normed, router_ref[...], (((1,), (1,)), ((), ())), preferred_element_type=F32
    )
    picked = jnp.where(place > 0.0, jax.nn.sigmoid(logits), 0.0)
    gate = picked / jnp.sum(picked, axis=1, keepdims=True)
    gate_hi = gate.astype(BF16)
    gate_lo = (gate - gate_hi.astype(F32)).astype(BF16)
    place = place.astype(BF16)
    for hi_ref, lo_ref, each in ((main_hi_ref, main_lo_ref, MAIN), (last_hi_ref, last_lo_ref, 1)):
        spread = widen(experts, 2 * each)
        lane = lax.broadcasted_iota(jnp.int32, hi_ref.shape, 1)
        core = lane // each % 2
        slot = core * HALF_CAP + (lane % each + 1 if each > 1 else HALF_CAP)
        here = dot(place, spread) == slot.astype(F32)
        hi_ref[...] = jnp.where(here, dot(gate_hi, spread), 0.0).astype(BF16)
        lo_ref[...] = jnp.where(here, dot(gate_lo, spread), 0.0).astype(BF16)


def ffn_kernel(*refs):
    stored, out_ref = refs[:17], refs[17]
    x_ref, last_ref, gate_ref, up_ref, act_ref, back_ref, ends_ref, rows_ref = refs[18:26]
    weights, sems, row_sem, out_sems = refs[26:42], refs[42], refs[43], refs[44]
    sections, _, part = x_ref.shape
    experts = rows_ref.shape[0]
    blocks = sections * part // LANES
    per = part // LANES
    main = experts * MAIN
    half = blocks // 2
    here = lax.axis_index("section").astype(jnp.int32)
    step = 256
    at = [lax.rem(here + d, sections) for d in (0, 1, 3, 2)]
    rows_in = pltpu.make_async_copy(stored[0], rows_ref, row_sem)
    copies = [pltpu.make_async_copy(stored[1 + i], weights[i], sems.at[i]) for i in range(16)]
    rows_in.start()
    for copy in copies[:AHEAD]:
        copy.start()
    rows_in.wait()
    last = rows_ref[:, blocks * MAIN :, :].astype(F32).reshape(experts, blocks * LANES)
    for s in range(sections):
        for c in range(per):
            b = s * per + c
            x_ref[s, :main, c * LANES : (c + 1) * LANES] = (
                rows_ref[:, b * MAIN : (b + 1) * MAIN, :].reshape(main, LANES)
            )
        x_ref[s, main:, :] = last[:, s * part : (s + 1) * part].astype(BF16)

    def piece(q, d, first, cols):
        edge = weights[0].shape[0]
        side, row = divmod(first, edge)
        return weights[q * 8 + d * 2 + side][row : row + step, cols]

    for q in range(2):
        for d in range(sections):
            for i in (q * 8 + d * 2, q * 8 + d * 2 + 1):
                copies[i].wait()
                if i + AHEAD < len(copies):
                    copies[i + AHEAD].start()
            for n in range(part // step):
                cols = slice(n * step, (n + 1) * step)
                totals = []
                for which, sum_ref in enumerate((gate_ref, up_ref)):
                    total = None if d == 0 else sum_ref[:, cols]
                    for k in range(part // step):
                        term = dot(
                            x_ref[at[d], :, k * step : (k + 1) * step],
                            piece(q, d, which * part + k * step, cols),
                        )
                        total = term if total is None else total + term
                    if d < sections - 1:
                        sum_ref[:, cols] = total
                    totals.append(total)
                if d == sections - 1:
                    act = jax.nn.silu(totals[0]) * totals[1]
                    act_ref[:, q * part + n * step : q * part + (n + 1) * step] = act.astype(BF16)
    outs = []
    for d in range(sections):
        wide = []
        for n in range(part // step):
            cols = slice(n * step, (n + 1) * step)
            total = None
            for q in range(2):
                partial = None
                for k in range(part // step):
                    term = dot(
                        act_ref[:, q * part + k * step : q * part + (k + 1) * step],
                        piece(q, d, 2 * part + k * step, cols),
                    )
                    partial = term if partial is None else partial + term
                partial = partial.astype(BF16).astype(F32)
                total = partial if total is None else total + partial
            for j in range(step // LANES):
                back_ref[d, :, n * (step // LANES) + j, :, :] = (
                    total[:main, j * LANES : (j + 1) * LANES]
                    .reshape(experts, MAIN, LANES)
                    .astype(BF16)
                )
            wide.append(total[main:])
        last_ref[at[d]] = jnp.concatenate(wide, axis=1).astype(BF16)
        span = pl.ds(at[d] % 2 * per, per)
        copy = pltpu.make_async_copy(
            back_ref.at[d], out_ref.at[:, at[d] // 2, span, :, :], out_sems.at[d]
        )
        copy.start()
        outs.append(copy)
    whole = jnp.concatenate([last_ref[s] for s in range(sections)], axis=1)
    whole = whole.astype(F32).reshape(experts, blocks, LANES).astype(BF16)
    for h in range(2):
        ends_ref[h] = whole[:, h * half : (h + 1) * half, :]
        copy = pltpu.make_async_copy(
            ends_ref.at[h], out_ref.at[:, h, half, :, :], out_sems.at[sections + h]
        )
        copy.start()
        outs.append(copy)
    for copy in outs:
        copy.wait()


def combine_kernel(
    rows_ref, mh_ref, ml_ref, lh_ref, ll_ref, state_ref, prelude_ref, inject_ref, out_ref
):
    width = out_ref.shape[1]
    senders = rows_ref.shape[0]
    half = width // LANES
    cols = pl.ds(pl.multiple_of(lax.axis_index("pair").astype(jnp.int32) * width, width), width)
    mixed = state_ref[:, cols].astype(F32) + prelude_ref[:, cols].astype(F32) * inject_ref[:, cols]
    last = rows_ref[:, half * MAIN :, :].astype(F32).reshape(senders, width).astype(BF16)
    mixed = mixed + (dot(lh_ref[...], last) + dot(ll_ref[...], last))
    for pair in range(half // 2):
        rows = [
            rows_ref[:, c * MAIN : (c + 1) * MAIN, :].reshape(senders * MAIN, LANES)
            for c in (2 * pair, 2 * pair + 1)
        ]
        rows = jnp.concatenate(rows, axis=1)
        span = slice(pair * 2 * LANES, (pair + 1) * 2 * LANES)
        moe = dot(mh_ref[...], rows) + dot(ml_ref[...], rows)
        out_ref[:, span] = (mixed[:, span] + moe).astype(BF16)


def call(kernel, outs, n_in, scratch=(), limit=10 << 20, far=False, far_outs=0):
    kinds = [FAR] * far_outs + [VMEM] * (len(outs) - far_outs)
    return pl.pallas_call(
        kernel,
        out_shape=outs,
        in_specs=[FAR if far else VMEM] * n_in,
        out_specs=tuple(kinds),
        scratch_shapes=list(scratch),
        compiler_params=pltpu.CompilerParams(vmem_limit_bytes=limit),
    )


def one_pass(initial_state, prelude, inject_gain, norm_gain, router, gate_w, up_w, down_w, routes):
    tokens, width = initial_state.shape
    experts = router.shape[1]
    blocks = width // LANES
    sections = lax.axis_size("section")
    part = gate_w.shape[1]
    inject = inject_gain[None, :]
    shape = jax.ShapeDtypeStruct
    dma = pltpu.SemaphoreType.DMA
    slots = experts * HALF_CAP

    message = shape((experts, blocks * HALF_CAP, LANES), BF16)
    piece = shape((3 * part // 2, part), BF16)
    inputs = (routes[0].T, initial_state, prelude, inject, norm_gain[None, :])
    send, own_lo, own_hi = call(
        route_kernel,
        (message, piece, piece),
        8,
        scratch=[
            pltpu.VMEM((TOPK, tokens), jnp.int32),
            pltpu.VMEM((tokens, width), BF16),
            pltpu.VMEM((tokens, width), BF16),
            pltpu.VMEM((1, width), F32),
            pltpu.VMEM((1, width), F32),
            pltpu.VMEM(message.shape, BF16),
            pltpu.VMEM((3 * part, part), BF16),
            dma((5,)),
            dma((3,)),
            dma((blocks // 2 + 1,)),
            dma((2,)),
        ],
        limit=WHOLE,
        far=True,
        far_outs=3,
    )(*inputs, gate_w[0], up_w[0], down_w[0])

    up_ring = [(i, (i + 1) % sections) for i in range(sections)]
    down_ring = [(i, (i - 1) % sections) for i in range(sections)]
    swap = [(0, 1), (1, 0)]

    before_lo = lax.ppermute(own_lo, "section", up_ring)
    after_hi = lax.ppermute(own_hi, "section", down_ring)
    before_hi = lax.ppermute(own_hi, "section", up_ring)
    after_lo = lax.ppermute(own_lo, "section", down_ring)
    far_lo = lax.ppermute(before_lo, "section", up_ring)
    far_hi = lax.ppermute(after_hi, "section", down_ring)
    mine = [own_lo, own_hi, after_lo, after_hi, before_lo, before_hi, far_lo, far_hi]
    other = [lax.ppermute(w, "pair", swap) for w in mine]

    received = lax.all_to_all(send, "expert", split_axis=0, concat_axis=0, tiled=True)
    (back,) = call(
        ffn_kernel,
        (shape((experts, 2, HALF_CAP, blocks // 2, LANES), BF16),),
        17,
        scratch=[
            pltpu.VMEM((sections, slots, part), BF16),
            pltpu.VMEM((sections, experts, part), BF16),
            pltpu.VMEM((slots, part), F32),
            pltpu.VMEM((slots, part), F32),
            pltpu.VMEM((slots, 2 * part), BF16),
            pltpu.VMEM((sections, experts, blocks // sections, MAIN, LANES), BF16),
            pltpu.VMEM((2, experts, blocks // 2, LANES), BF16),
            pltpu.VMEM(message.shape, BF16),
            *[pltpu.VMEM(w.shape, BF16) for w in mine + other],
            dma((16,)),
            dma,
            dma((sections + 2,)),
        ],
        limit=WHOLE,
        far=True,
        far_outs=1,
    )(received, *mine, *other)
    weights = call(
        gate_kernel,
        (shape((tokens, 2 * experts * MAIN), BF16),) * 2
        + (shape((tokens, 2 * experts), BF16),) * 2,
        6,
    )(*inputs, router.T)
    back = back.reshape(2 * experts, blocks // 2 * HALF_CAP, LANES)
    returned = lax.all_to_all(back, ("expert", "pair"), split_axis=0, concat_axis=0, tiled=True)
    (out,) = call(combine_kernel, (shape((tokens, width // 2), BF16),), 8)(
        returned, *weights, initial_state, prelude, inject
    )
    return out


def solution(mesh):
    placed = (
        P(("section", "expert"), None),
        P(("section", "expert"), None),
        P(),
        P(),
        P(),
        P("expert", "section", "pair"),
        P("expert", "section", "pair"),
        P("expert", "pair", "section"),
        P(None, ("section", "expert"), None),
    )
    return jax.shard_map(
        one_pass,
        mesh=mesh,
        in_specs=placed,
        out_specs=P(("section", "expert"), "pair"),
        check_vma=False,
    )
```

```python
import jax
import jax.numpy as jnp
from jax import lax
from jax.experimental import pallas as pl
from jax.experimental.pallas import tpu as pltpu
from jax.sharding import PartitionSpec as P


TOPK = 8
CAP = 18
MAIN = 8
HALF_CAP = CAP // 2
LANES = 128
AHEAD = 4
WHOLE = 67_000_000
F32 = jnp.float32
BF16 = jnp.bfloat16
VMEM = pl.BlockSpec(memory_space=pltpu.VMEM)
FAR = pl.BlockSpec(memory_space=pltpu.HBM)


def dot(a, b):
    return jnp.dot(a, b, preferred_element_type=F32)


def dot_t(a, b):
    return lax.dot_general(a, b, (((0,), (0,)), ((), ())), preferred_element_type=F32)


def normalize(state, prelude, inject, gain):
    mixed = state.astype(F32) + prelude.astype(F32) * inject
    inv_rms = lax.rsqrt(jnp.mean(mixed * mixed, axis=-1, keepdims=True) + 1e-06)
    return (mixed * inv_rms * gain).astype(BF16)


def places(routes, experts):
    routes = routes.astype(F32).T.astype(jnp.int32)
    tokens = routes.shape[0]
    expert = lax.broadcasted_iota(jnp.int32, (tokens, experts), 1)
    chosen = routes[:, 0:1] == expert
    for k in range(1, TOPK):
        chosen = jnp.logical_or(chosen, routes[:, k : k + 1] == expert)
    earlier = lax.broadcasted_iota(jnp.int32, (tokens, tokens), 1) < lax.broadcasted_iota(
        jnp.int32, (tokens, tokens), 0
    )
    rank = dot(earlier.astype(F32).astype(BF16), chosen.astype(F32).astype(BF16))
    return jnp.where(chosen, rank + 1.0, 0.0)


def widen(rows, times):
    lane = lax.broadcasted_iota(jnp.int32, (rows, rows * times), 1)
    row = lax.broadcasted_iota(jnp.int32, (rows, rows * times), 0)
    return (lane // times == row).astype(F32).astype(BF16)


def route_kernel(*refs):
    stored, parts, out_ref, own_ref = refs[:5], refs[5:8], refs[8], refs[9]
    held, send_ref, pack_ref, sems, pack_sems, out_sems, own_sem = (
        refs[10:15], refs[15], refs[16], refs[17], refs[18], refs[19], refs[20],
    )
    copies = [pltpu.make_async_copy(stored[i], held[i], sems.at[i]) for i in range(5)]
    for copy in copies:
        copy.start()
    size = parts[0].shape[0]
    packs = [
        pltpu.make_async_copy(parts[i], pack_ref.at[i * size : (i + 1) * size], pack_sems.at[i])
        for i in range(3)
    ]
    for copy in packs:
        copy.start()
    routes_ref, state_ref, prelude_ref, inject_ref, gain_ref = held
    width = state_ref.shape[1]
    experts = send_ref.shape[0]
    blocks = width // LANES
    low = lax.axis_index("pair").astype(jnp.int32) * HALF_CAP
    copies[0].wait()
    place = places(routes_ref[...], experts)
    slot = lax.broadcasted_iota(jnp.int32, (place.shape[0], experts * MAIN), 1) % MAIN + (1 + low)
    at_main = dot(place.astype(BF16), widen(experts, MAIN)) == slot.astype(F32)
    at_last = place == (low + HALF_CAP).astype(F32)
    pick_main = at_main.astype(F32).astype(BF16)
    pick_last = at_last.astype(F32).astype(BF16)
    for copy in copies[1:]:
        copy.wait()
    normed = normalize(state_ref[...], prelude_ref[...], inject_ref[...], gain_ref[...])
    outs = []

    def give(first, size):
        copy = pltpu.make_async_copy(
            send_ref.at[:, first : first + size, :],
            out_ref.at[:, first : first + size, :],
            out_sems.at[len(outs)],
        )
        copy.start()
        outs.append(copy)

    last = dot_t(pick_last, normed)
    send_ref[:, blocks * MAIN :, :] = last.reshape(experts, blocks, LANES).astype(BF16)
    give(blocks * MAIN, blocks)
    for pair in range(blocks // 2):
        cols = normed[:, pair * 2 * LANES : (pair + 1) * 2 * LANES]
        rows = dot_t(pick_main, cols)
        for j in range(2):
            c = 2 * pair + j
            send_ref[:, c * MAIN : (c + 1) * MAIN, :] = (
                rows[:, j * LANES : (j + 1) * LANES].reshape(experts, MAIN, LANES).astype(BF16)
            )
        give(pair * 2 * MAIN, 2 * MAIN)
        if pair == 0:
            for copy in packs:
                copy.wait()
            own = pltpu.make_async_copy(pack_ref, own_ref, own_sem)
            own.start()
    own.wait()
    for copy in outs:
        copy.wait()


def gate_kernel(
    routes_ref, state_ref, prelude_ref, inject_ref, gain_ref, router_ref,
    main_hi_ref, main_lo_ref, last_hi_ref, last_lo_ref,
):
    experts = router_ref.shape[0]
    place = places(routes_ref[...], experts)
    normed = normalize(state_ref[...], prelude_ref[...], inject_ref[...], gain_ref[...])
    logits = lax.dot_general(
        normed, router_ref[...], (((1,), (1,)), ((), ())), preferred_element_type=F32
    )
    picked = jnp.where(place > 0.0, jax.nn.sigmoid(logits), 0.0)
    gate = picked / jnp.sum(picked, axis=1, keepdims=True)
    gate_hi = gate.astype(BF16)
    gate_lo = (gate - gate_hi.astype(F32)).astype(BF16)
    place = place.astype(BF16)
    for hi_ref, lo_ref, each in ((main_hi_ref, main_lo_ref, MAIN), (last_hi_ref, last_lo_ref, 1)):
        spread = widen(experts, 2 * each)
        lane = lax.broadcasted_iota(jnp.int32, hi_ref.shape, 1)
        core = lane // each % 2
        slot = core * HALF_CAP + (lane % each + 1 if each > 1 else HALF_CAP)
        here = dot(place, spread) == slot.astype(F32)
        hi_ref[...] = jnp.where(here, dot(gate_hi, spread), 0.0).astype(BF16)
        lo_ref[...] = jnp.where(here, dot(gate_lo, spread), 0.0).astype(BF16)


def ffn_kernel(*refs):
    stored, out_ref = refs[:9], refs[9]
    x_ref, last_ref, gate_ref, up_ref, act_ref, back_ref, ends_ref, rows_ref = refs[10:18]
    weights, sems, row_sem, out_sems = refs[18:26], refs[26], refs[27], refs[28]
    sections, _, part = x_ref.shape
    experts = rows_ref.shape[0]
    blocks = sections * part // LANES
    per = part // LANES
    main = experts * MAIN
    half = blocks // 2
    here = lax.axis_index("section").astype(jnp.int32)
    step = 256
    turn = 1 - 2 * lax.axis_index("pair").astype(jnp.int32)
    steps = (0, sections - turn, sections + turn, 2)
    at = [lax.rem(here + d, sections) for d in steps]
    same = (0, 2, 1, 3)
    cut = weights[0].shape[0] // 2
    rows_in = pltpu.make_async_copy(stored[0], rows_ref, row_sem)
    copies = [
        pltpu.make_async_copy(
            stored[1 + i // 2].at[i % 2 * cut : (i % 2 + 1) * cut],
            weights[i // 2].at[i % 2 * cut : (i % 2 + 1) * cut],
            sems.at[i],
        )
        for i in range(16)
    ]
    rows_in.start()
    for copy in copies[:AHEAD]:
        copy.start()
    rows_in.wait()
    last = rows_ref[:, blocks * MAIN :, :].astype(F32).reshape(experts, blocks * LANES)
    for s in range(sections):
        for c in range(per):
            b = s * per + c
            x_ref[s, :main, c * LANES : (c + 1) * LANES] = (
                rows_ref[:, b * MAIN : (b + 1) * MAIN, :].reshape(main, LANES)
            )
        x_ref[s, main:, :] = last[:, s * part : (s + 1) * part].astype(BF16)

    def piece(q, d, first, cols):
        return weights[q * 4 + d][first : first + step, cols]

    for q in range(2):
        for d in range(sections):
            for i in (q * 8 + d * 2, q * 8 + d * 2 + 1):
                copies[i].wait()
                if i + AHEAD < len(copies):
                    copies[i + AHEAD].start()
            for n in range(part // step):
                cols = slice(n * step, (n + 1) * step)
                totals = []
                for which, sum_ref in enumerate((gate_ref, up_ref)):
                    total = None if d == 0 else sum_ref[:, cols]
                    for k in range(part // step):
                        term = dot(
                            x_ref[at[d if q == 0 else same[d]], :, k * step : (k + 1) * step],
                            piece(q, d, which * part + k * step, cols),
                        )
                        total = term if total is None else total + term
                    if d < sections - 1:
                        sum_ref[:, cols] = total
                    totals.append(total)
                if d == sections - 1:
                    act = jax.nn.silu(totals[0]) * totals[1]
                    act_ref[:, q * part + n * step : q * part + (n + 1) * step] = act.astype(BF16)
    outs = []
    for d in range(sections):
        wide = []
        for n in range(part // step):
            cols = slice(n * step, (n + 1) * step)
            total = None
            for q in range(2):
                partial = None
                for k in range(part // step):
                    term = dot(
                        act_ref[:, q * part + k * step : q * part + (k + 1) * step],
                        piece(q, d if q == 0 else same[d], 2 * part + k * step, cols),
                    )
                    partial = term if partial is None else partial + term
                partial = partial.astype(BF16).astype(F32)
                total = partial if total is None else total + partial
            for j in range(step // LANES):
                back_ref[d, :, n * (step // LANES) + j, :, :] = (
                    total[:main, j * LANES : (j + 1) * LANES]
                    .reshape(experts, MAIN, LANES)
                    .astype(BF16)
                )
            wide.append(total[main:])
        last_ref[at[d]] = jnp.concatenate(wide, axis=1).astype(BF16)
        span = pl.ds(at[d] % 2 * per, per)
        copy = pltpu.make_async_copy(
            back_ref.at[d], out_ref.at[:, at[d] // 2, span, :, :], out_sems.at[d]
        )
        copy.start()
        outs.append(copy)
    whole = jnp.concatenate([last_ref[s] for s in range(sections)], axis=1)
    whole = whole.astype(F32).reshape(experts, blocks, LANES).astype(BF16)
    for h in range(2):
        ends_ref[h] = whole[:, h * half : (h + 1) * half, :]
        copy = pltpu.make_async_copy(
            ends_ref.at[h], out_ref.at[:, h, half, :, :], out_sems.at[sections + h]
        )
        copy.start()
        outs.append(copy)
    for copy in outs:
        copy.wait()


def combine_kernel(
    rows_ref, mh_ref, ml_ref, lh_ref, ll_ref, state_ref, prelude_ref, inject_ref, out_ref
):
    width = out_ref.shape[1]
    senders = rows_ref.shape[0]
    half = width // LANES
    cols = pl.ds(pl.multiple_of(lax.axis_index("pair").astype(jnp.int32) * width, width), width)
    mixed = state_ref[:, cols].astype(F32) + prelude_ref[:, cols].astype(F32) * inject_ref[:, cols]
    last = rows_ref[:, half * MAIN :, :].astype(F32).reshape(senders, width).astype(BF16)
    mixed = mixed + (dot(lh_ref[...], last) + dot(ll_ref[...], last))
    for pair in range(half // 2):
        rows = [
            rows_ref[:, c * MAIN : (c + 1) * MAIN, :].reshape(senders * MAIN, LANES)
            for c in (2 * pair, 2 * pair + 1)
        ]
        rows = jnp.concatenate(rows, axis=1)
        span = slice(pair * 2 * LANES, (pair + 1) * 2 * LANES)
        moe = dot(mh_ref[...], rows) + dot(ml_ref[...], rows)
        out_ref[:, span] = (mixed[:, span] + moe).astype(BF16)


def call(kernel, outs, n_in, scratch=(), limit=10 << 20, far=False, far_outs=0):
    kinds = [FAR] * far_outs + [VMEM] * (len(outs) - far_outs)
    return pl.pallas_call(
        kernel,
        out_shape=outs,
        in_specs=[FAR if far else VMEM] * n_in,
        out_specs=tuple(kinds),
        scratch_shapes=list(scratch),
        compiler_params=pltpu.CompilerParams(vmem_limit_bytes=limit),
    )


def one_pass(initial_state, prelude, inject_gain, norm_gain, router, gate_w, up_w, down_w, routes):
    tokens, width = initial_state.shape
    experts = router.shape[1]
    blocks = width // LANES
    sections = lax.axis_size("section")
    part = gate_w.shape[1]
    inject = inject_gain[None, :]
    shape = jax.ShapeDtypeStruct
    dma = pltpu.SemaphoreType.DMA
    slots = experts * HALF_CAP

    message = shape((experts, blocks * HALF_CAP, LANES), BF16)
    piece = shape((3 * part, part), BF16)
    inputs = (routes[0].T, initial_state, prelude, inject, norm_gain[None, :])
    send, own = call(
        route_kernel,
        (message, piece),
        8,
        scratch=[
            pltpu.VMEM((TOPK, tokens), jnp.int32),
            pltpu.VMEM((tokens, width), BF16),
            pltpu.VMEM((tokens, width), BF16),
            pltpu.VMEM((1, width), F32),
            pltpu.VMEM((1, width), F32),
            pltpu.VMEM(message.shape, BF16),
            pltpu.VMEM((3 * part, part), BF16),
            dma((5,)),
            dma((3,)),
            dma((blocks // 2 + 1,)),
            dma,
        ],
        limit=WHOLE,
        far=True,
        far_outs=2,
    )(*inputs, gate_w[0], up_w[0], down_w[0])

    def ring(turn):
        return [
            (2 * i + p, (i + turn * (1 - 2 * p)) % sections * 2 + p)
            for i in range(sections)
            for p in range(2)
        ]

    near = lax.ppermute(own, ("section", "pair"), ring(1))
    back_near = lax.ppermute(own, ("section", "pair"), ring(-1))
    far = lax.ppermute(near, ("section", "pair"), ring(1))
    mine = [own, near, back_near, far]
    other = [lax.ppermute(w, "pair", [(0, 1), (1, 0)]) for w in mine]

    received = lax.all_to_all(send, "expert", split_axis=0, concat_axis=0, tiled=True)
    (back,) = call(
        ffn_kernel,
        (shape((experts, 2, HALF_CAP, blocks // 2, LANES), BF16),),
        9,
        scratch=[
            pltpu.VMEM((sections, slots, part), BF16),
            pltpu.VMEM((sections, experts, part), BF16),
            pltpu.VMEM((slots, part), F32),
            pltpu.VMEM((slots, part), F32),
            pltpu.VMEM((slots, 2 * part), BF16),
            pltpu.VMEM((sections, experts, blocks // sections, MAIN, LANES), BF16),
            pltpu.VMEM((2, experts, blocks // 2, LANES), BF16),
            pltpu.VMEM(message.shape, BF16),
            *[pltpu.VMEM(w.shape, BF16) for w in mine + other],
            dma((16,)),
            dma,
            dma((sections + 2,)),
        ],
        limit=WHOLE,
        far=True,
        far_outs=1,
    )(received, *mine, *other)
    weights = call(
        gate_kernel,
        (shape((tokens, 2 * experts * MAIN), BF16),) * 2
        + (shape((tokens, 2 * experts), BF16),) * 2,
        6,
    )(*inputs, router.T)
    back = back.reshape(2 * experts, blocks // 2 * HALF_CAP, LANES)
    returned = lax.all_to_all(back, ("expert", "pair"), split_axis=0, concat_axis=0, tiled=True)
    (out,) = call(combine_kernel, (shape((tokens, width // 2), BF16),), 8)(
        returned, *weights, initial_state, prelude, inject
    )
    return out


def solution(mesh):
    placed = (
        P(("section", "expert"), None),
        P(("section", "expert"), None),
        P(),
        P(),
        P(),
        P("expert", "section", "pair"),
        P("expert", "section", "pair"),
        P("expert", "pair", "section"),
        P(None, ("section", "expert"), None),
    )
    return jax.shard_map(
        one_pass,
        mesh=mesh,
        in_specs=placed,
        out_specs=P(("section", "expert"), "pair"),
        check_vma=False,
    )
```

```python
import jax
import jax.numpy as jnp
from jax import lax
from jax.experimental import pallas as pl
from jax.experimental.pallas import tpu as pltpu
from jax.sharding import PartitionSpec as P


TOPK = 8
CAP = 18
MAIN = 8
HALF_CAP = CAP // 2
LANES = 128
AHEAD = 4
WHOLE = 67_000_000
F32 = jnp.float32
BF16 = jnp.bfloat16
VMEM = pl.BlockSpec(memory_space=pltpu.VMEM)
FAR = pl.BlockSpec(memory_space=pltpu.HBM)


def dot(a, b):
    return jnp.dot(a, b, preferred_element_type=F32)


def dot_t(a, b):
    return lax.dot_general(a, b, (((0,), (0,)), ((), ())), preferred_element_type=F32)


def normalize(state, prelude, inject, gain):
    mixed = state.astype(F32) + prelude.astype(F32) * inject
    inv_rms = lax.rsqrt(jnp.mean(mixed * mixed, axis=-1, keepdims=True) + 1e-06)
    return (mixed * inv_rms * gain).astype(BF16)


def places(routes, experts):
    routes = routes.astype(F32).T.astype(jnp.int32)
    tokens = routes.shape[0]
    expert = lax.broadcasted_iota(jnp.int32, (tokens, experts), 1)
    chosen = routes[:, 0:1] == expert
    for k in range(1, TOPK):
        chosen = jnp.logical_or(chosen, routes[:, k : k + 1] == expert)
    earlier = lax.broadcasted_iota(jnp.int32, (tokens, tokens), 1) < lax.broadcasted_iota(
        jnp.int32, (tokens, tokens), 0
    )
    rank = dot(earlier.astype(F32).astype(BF16), chosen.astype(F32).astype(BF16))
    return jnp.where(chosen, rank + 1.0, 0.0)


def widen(rows, times):
    lane = lax.broadcasted_iota(jnp.int32, (rows, rows * times), 1)
    row = lax.broadcasted_iota(jnp.int32, (rows, rows * times), 0)
    return (lane // times == row).astype(F32).astype(BF16)


def route_kernel(*refs):
    stored, parts, out_ref, own_ref = refs[:5], refs[5:8], refs[8], refs[9]
    held, send_ref, pack_ref, sems, pack_sems, out_sems, own_sem = (
        refs[10:15], refs[15], refs[16], refs[17], refs[18], refs[19], refs[20],
    )
    copies = [pltpu.make_async_copy(stored[i], held[i], sems.at[i]) for i in range(5)]
    for copy in copies:
        copy.start()
    size = parts[0].shape[0]
    packs = [
        pltpu.make_async_copy(parts[i], pack_ref.at[i * size : (i + 1) * size], pack_sems.at[i])
        for i in range(3)
    ]
    for copy in packs:
        copy.start()
    routes_ref, state_ref, prelude_ref, inject_ref, gain_ref = held
    width = state_ref.shape[1]
    experts = send_ref.shape[0]
    blocks = width // LANES
    low = lax.axis_index("pair").astype(jnp.int32) * HALF_CAP
    copies[0].wait()
    place = places(routes_ref[...], experts)
    slot = lax.broadcasted_iota(jnp.int32, (place.shape[0], experts * MAIN), 1) % MAIN + (1 + low)
    at_main = dot(place.astype(BF16), widen(experts, MAIN)) == slot.astype(F32)
    at_last = place == (low + HALF_CAP).astype(F32)
    pick_main = at_main.astype(F32).astype(BF16)
    pick_last = at_last.astype(F32).astype(BF16)
    for copy in copies[1:]:
        copy.wait()
    normed = normalize(state_ref[...], prelude_ref[...], inject_ref[...], gain_ref[...])
    outs = []

    def give(first, size):
        copy = pltpu.make_async_copy(
            send_ref.at[:, first : first + size, :],
            out_ref.at[:, first : first + size, :],
            out_sems.at[len(outs)],
        )
        copy.start()
        outs.append(copy)

    last = dot_t(pick_last, normed)
    send_ref[:, blocks * MAIN :, :] = last.reshape(experts, blocks, LANES).astype(BF16)
    give(blocks * MAIN, blocks)
    for pair in range(blocks // 2):
        cols = normed[:, pair * 2 * LANES : (pair + 1) * 2 * LANES]
        rows = dot_t(pick_main, cols)
        for j in range(2):
            c = 2 * pair + j
            send_ref[:, c * MAIN : (c + 1) * MAIN, :] = (
                rows[:, j * LANES : (j + 1) * LANES].reshape(experts, MAIN, LANES).astype(BF16)
            )
        give(pair * 2 * MAIN, 2 * MAIN)
        if pair == 0:
            for copy in packs:
                copy.wait()
            own = pltpu.make_async_copy(pack_ref, own_ref, own_sem)
            own.start()
    own.wait()
    for copy in outs:
        copy.wait()


def gate_kernel(
    routes_ref, state_ref, prelude_ref, inject_ref, gain_ref, router_ref,
    main_ref, last_ref,
):
    tokens, experts = state_ref.shape[0], router_ref.shape[0]
    place = places(routes_ref[...], experts)
    normed = normalize(state_ref[...], prelude_ref[...], inject_ref[...], gain_ref[...])
    logits = lax.dot_general(
        normed, router_ref[...], (((1,), (1,)), ((), ())), preferred_element_type=F32
    )
    picked = jnp.where(place > 0.0, jax.nn.sigmoid(logits), 0.0)
    gate = picked / jnp.sum(picked, axis=1, keepdims=True)
    gate_hi = gate.astype(BF16)
    gate_lo = (gate - gate_hi.astype(F32)).astype(BF16)
    place = place.astype(BF16)
    for out_ref, each in ((main_ref, MAIN), (last_ref, 1)):
        spread = widen(experts, 2 * each)
        lane = lax.broadcasted_iota(jnp.int32, (tokens, out_ref.shape[1]), 1)
        core = lane // each % 2
        slot = core * HALF_CAP + (lane % each + 1 if each > 1 else HALF_CAP)
        here = dot(place, spread) == slot.astype(F32)
        out_ref[:tokens] = jnp.where(here, dot(gate_hi, spread), 0.0).astype(BF16)
        out_ref[tokens:] = jnp.where(here, dot(gate_lo, spread), 0.0).astype(BF16)


def ffn_kernel(*refs):
    stored, out_ref = refs[:9], refs[9]
    x_ref, last_ref, gate_ref, up_ref, act_ref, back_ref, ends_ref = refs[10:17]
    rows_ref, first_ref, weights, sems, row_sems, out_sems = (
        refs[17], refs[18], refs[19:27], refs[27], refs[28], refs[29],
    )
    sections, _, part = x_ref.shape
    experts = rows_ref.shape[1]
    blocks = sections * part // LANES
    per = part // LANES
    main = experts * MAIN
    half = blocks // 2
    here = lax.axis_index("section").astype(jnp.int32)
    step = 256
    turn = 1 - 2 * lax.axis_index("pair").astype(jnp.int32)
    steps = (0, sections - turn, sections + turn, 2)
    at = [lax.rem(here + d, sections) for d in steps]
    same = (0, 2, 1, 3)
    cut = weights[0].shape[0] // 2
    spans = [pl.ds(pl.multiple_of(a * (per * MAIN), per * MAIN), per * MAIN) for a in at]
    rows_in = [
        pltpu.make_async_copy(stored[0].at[:, span, :], rows_ref.at[d], row_sems.at[d])
        for d, span in enumerate(spans)
    ]
    ends_in = pltpu.make_async_copy(
        stored[0].at[:, blocks * MAIN :, :], first_ref, row_sems.at[sections]
    )
    copies = [
        pltpu.make_async_copy(
            stored[1 + i // 2].at[i % 2 * cut : (i % 2 + 1) * cut],
            weights[i // 2].at[i % 2 * cut : (i % 2 + 1) * cut],
            sems.at[i],
        )
        for i in range(16)
    ]
    ends_in.start()
    rows_in[0].start()
    for copy in copies[:2]:
        copy.start()
    for copy in rows_in[1:]:
        copy.start()
    for copy in copies[2:AHEAD]:
        copy.start()
    ends_in.wait()
    last = first_ref[...].astype(F32).reshape(experts, blocks * LANES)
    for s in range(sections):
        last_ref[s] = last[:, s * part : (s + 1) * part].astype(BF16)

    def piece(q, d, first, cols):
        return weights[q * 4 + d][first : first + step, cols]

    for q in range(2):
        for d in range(sections):
            if q == 0:
                rows_in[d].wait()
                for c in range(per):
                    x_ref[d, :main, c * LANES : (c + 1) * LANES] = (
                        rows_ref[d, :, c * MAIN : (c + 1) * MAIN, :].reshape(main, LANES)
                    )
                x_ref[d, main:, :] = last_ref[at[d]]
            for i in (q * 8 + d * 2, q * 8 + d * 2 + 1):
                copies[i].wait()
                if i + AHEAD < len(copies):
                    copies[i + AHEAD].start()
            for n in range(part // step):
                cols = slice(n * step, (n + 1) * step)
                totals = []
                for which, sum_ref in enumerate((gate_ref, up_ref)):
                    total = None if d == 0 else sum_ref[:, cols]
                    for k in range(part // step):
                        term = dot(
                            x_ref[d if q == 0 else same[d], :, k * step : (k + 1) * step],
                            piece(q, d, which * part + k * step, cols),
                        )
                        total = term if total is None else total + term
                    if d < sections - 1:
                        sum_ref[:, cols] = total
                    totals.append(total)
                if d == sections - 1:
                    act = jax.nn.silu(totals[0]) * totals[1]
                    act_ref[:, q * part + n * step : q * part + (n + 1) * step] = act.astype(BF16)
    outs = []
    for d in range(sections):
        wide = []
        for n in range(part // step):
            cols = slice(n * step, (n + 1) * step)
            total = None
            for q in range(2):
                partial = None
                for k in range(part // step):
                    term = dot(
                        act_ref[:, q * part + k * step : q * part + (k + 1) * step],
                        piece(q, d if q == 0 else same[d], 2 * part + k * step, cols),
                    )
                    partial = term if partial is None else partial + term
                partial = partial.astype(BF16).astype(F32)
                total = partial if total is None else total + partial
            for j in range(step // LANES):
                back_ref[d, :, n * (step // LANES) + j, :, :] = (
                    total[:main, j * LANES : (j + 1) * LANES]
                    .reshape(experts, MAIN, LANES)
                    .astype(BF16)
                )
            wide.append(total[main:])
        last_ref[at[d]] = jnp.concatenate(wide, axis=1).astype(BF16)
        span = pl.ds(at[d] % 2 * per, per)
        copy = pltpu.make_async_copy(
            back_ref.at[d], out_ref.at[:, at[d] // 2, span, :, :], out_sems.at[d]
        )
        copy.start()
        outs.append(copy)
    whole = jnp.concatenate([last_ref[s] for s in range(sections)], axis=1)
    whole = whole.astype(F32).reshape(experts, blocks, LANES).astype(BF16)
    for h in range(2):
        ends_ref[h] = whole[:, h * half : (h + 1) * half, :]
        copy = pltpu.make_async_copy(
            ends_ref.at[h], out_ref.at[:, h, half, :, :], out_sems.at[sections + h]
        )
        copy.start()
        outs.append(copy)
    for copy in outs:
        copy.wait()


def combine_kernel(rows_ref, main_ref, ends_ref, state_ref, prelude_ref, inject_ref, out_ref):
    tokens, width = out_ref.shape
    senders = rows_ref.shape[0]
    half = width // LANES

    def weigh(weights, rows):
        both = dot(weights, rows)
        return both[:tokens] + both[tokens:]

    cols = pl.ds(pl.multiple_of(lax.axis_index("pair").astype(jnp.int32) * width, width), width)
    mixed = state_ref[:, cols].astype(F32) + prelude_ref[:, cols].astype(F32) * inject_ref[:, cols]
    last = rows_ref[:, half * MAIN :, :].astype(F32).reshape(senders, width).astype(BF16)
    mixed = mixed + weigh(ends_ref[...], last)
    for pair in range(half // 2):
        rows = [
            rows_ref[:, c * MAIN : (c + 1) * MAIN, :].reshape(senders * MAIN, LANES)
            for c in (2 * pair, 2 * pair + 1)
        ]
        rows = jnp.concatenate(rows, axis=1)
        span = slice(pair * 2 * LANES, (pair + 1) * 2 * LANES)
        out_ref[:, span] = (mixed[:, span] + weigh(main_ref[...], rows)).astype(BF16)


def call(kernel, outs, n_in, scratch=(), limit=10 << 20, far=False, far_outs=0):
    kinds = [FAR] * far_outs + [VMEM] * (len(outs) - far_outs)
    return pl.pallas_call(
        kernel,
        out_shape=outs,
        in_specs=[FAR if far else VMEM] * n_in,
        out_specs=tuple(kinds),
        scratch_shapes=list(scratch),
        compiler_params=pltpu.CompilerParams(vmem_limit_bytes=limit),
    )


def one_pass(initial_state, prelude, inject_gain, norm_gain, router, gate_w, up_w, down_w, routes):
    tokens, width = initial_state.shape
    experts = router.shape[1]
    blocks = width // LANES
    sections = lax.axis_size("section")
    part = gate_w.shape[1]
    inject = inject_gain[None, :]
    shape = jax.ShapeDtypeStruct
    dma = pltpu.SemaphoreType.DMA
    slots = experts * HALF_CAP

    message = shape((experts, blocks * HALF_CAP, LANES), BF16)
    piece = shape((3 * part, part), BF16)
    inputs = (routes[0].T, initial_state, prelude, inject, norm_gain[None, :])
    send, own = call(
        route_kernel,
        (message, piece),
        8,
        scratch=[
            pltpu.VMEM((TOPK, tokens), jnp.int32),
            pltpu.VMEM((tokens, width), BF16),
            pltpu.VMEM((tokens, width), BF16),
            pltpu.VMEM((1, width), F32),
            pltpu.VMEM((1, width), F32),
            pltpu.VMEM(message.shape, BF16),
            pltpu.VMEM((3 * part, part), BF16),
            dma((5,)),
            dma((3,)),
            dma((blocks // 2 + 1,)),
            dma,
        ],
        limit=WHOLE,
        far=True,
        far_outs=2,
    )(*inputs, gate_w[0], up_w[0], down_w[0])

    def ring(turn):
        return [
            (2 * i + p, (i + turn * (1 - 2 * p)) % sections * 2 + p)
            for i in range(sections)
            for p in range(2)
        ]

    near = lax.ppermute(own, ("section", "pair"), ring(1))
    back_near = lax.ppermute(own, ("section", "pair"), ring(-1))
    far = lax.ppermute(near, ("section", "pair"), ring(1))
    mine = [own, near, back_near, far]
    other = [lax.ppermute(w, "pair", [(0, 1), (1, 0)]) for w in mine]

    received = lax.all_to_all(send, "expert", split_axis=0, concat_axis=0, tiled=True)
    (back,) = call(
        ffn_kernel,
        (shape((experts, 2, HALF_CAP, blocks // 2, LANES), BF16),),
        9,
        scratch=[
            pltpu.VMEM((sections, slots, part), BF16),
            pltpu.VMEM((sections, experts, part), BF16),
            pltpu.VMEM((slots, part), F32),
            pltpu.VMEM((slots, part), F32),
            pltpu.VMEM((slots, 2 * part), BF16),
            pltpu.VMEM((sections, experts, blocks // sections, MAIN, LANES), BF16),
            pltpu.VMEM((2, experts, blocks // 2, LANES), BF16),
            pltpu.VMEM((sections, experts, blocks // sections * MAIN, LANES), BF16),
            pltpu.VMEM((experts, blocks, LANES), BF16),
            *[pltpu.VMEM(w.shape, BF16) for w in mine + other],
            dma((16,)),
            dma((sections + 1,)),
            dma((sections + 2,)),
        ],
        limit=WHOLE,
        far=True,
        far_outs=1,
    )(received, *mine, *other)
    weights = call(
        gate_kernel,
        (
            shape((2 * tokens, 2 * experts * MAIN), BF16),
            shape((2 * tokens, 2 * experts), BF16),
        ),
        6,
    )(*inputs, router.T)
    back = back.reshape(2 * experts, blocks // 2 * HALF_CAP, LANES)
    returned = lax.all_to_all(back, ("expert", "pair"), split_axis=0, concat_axis=0, tiled=True)
    (out,) = call(combine_kernel, (shape((tokens, width // 2), BF16),), 6)(
        returned, *weights, initial_state, prelude, inject
    )
    return out


def solution(mesh):
    placed = (
        P(("section", "expert"), None),
        P(("section", "expert"), None),
        P(),
        P(),
        P(),
        P("expert", "section", "pair"),
        P("expert", "section", "pair"),
        P("expert", "pair", "section"),
        P(None, ("section", "expert"), None),
    )
    return jax.shard_map(
        one_pass,
        mesh=mesh,
        in_specs=placed,
        out_specs=P(("section", "expert"), "pair"),
        check_vma=False,
    )
```
